32 devices in a mesh: rhombus: 4 (over z), tile: 8 (over y, x, core).
Axes of the slice: x: 2, y: 2, z: 4, core: 2. Of those that a mesh axis runs over, the one named last changes fastest.
Arguments:
- fine_latent: bfloat16 [16384, 512], P(('rhombus', 'tile')), may hold values from -6 to 6
- mid_latent: bfloat16 [1024, 512], P(('rhombus', 'tile')), may hold values from -6 to 6
- coarse_latent: bfloat16 [642, 512], replicated, may hold values from -6 to 6
- fine_parent: int32 [16384], P(('rhombus', 'tile')), may hold values from 0 to 95, as said below
- mid_parent: int32 [1024], P(('rhombus', 'tile')), may hold values from 0 to 641
- halo_rows: int32 [8192], P(('rhombus', 'tile')), may hold values from 0 to 511
- edge_source: int32 [98304], P(('rhombus', 'tile')), may hold values from 0 to 767
- edge_target: int32 [98304], P(('rhombus', 'tile')), may hold values from 0 to 512, as said below
- w_child: bfloat16 [512, 512], replicated, may hold values from -1 to 1
- mid_w1: bfloat16 [512, 512], replicated, may hold values from -0.25 to 0.25
- mid_w2: bfloat16 [512, 512], replicated, may hold values from -0.5 to 0.5
- mid_w3: bfloat16 [512, 512], replicated, may hold values from -0.25 to 0.25
- w_coarse: bfloat16 [512, 512], replicated, may hold values from -1 to 1
- coarse_w1: bfloat16 [512, 512], replicated, may hold values from -0.25 to 0.25
- coarse_w2: bfloat16 [512, 512], replicated, may hold values from -0.5 to 0.5
- coarse_w3: bfloat16 [512, 512], replicated, may hold values from -0.25 to 0.25
- w_descend: bfloat16 [512, 512], replicated, may hold values from -0.25 to 0.25
- w_fine: bfloat16 [512, 512], replicated, may hold values from -0.25 to 0.25
- edge_w_src: bfloat16 [512, 512], replicated, may hold values from -1 to 1
- edge_w_dst: bfloat16 [512, 512], replicated, may hold values from -0.25 to 0.25
- edge_w2: bfloat16 [512, 512], replicated, may hold values from -0.25 to 0.25
- node_w1: bfloat16 [512, 512], replicated, may hold values from -0.25 to 0.25
- node_w2: bfloat16 [512, 512], replicated, may hold values from -0.125 to 0.125
- node_w3: bfloat16 [512, 512], replicated, may hold values from -0.25 to 0.25
Outputs:
- fine_out: bfloat16 [16384, 512], P(('rhombus', 'tile'))
- mid_out: bfloat16 [1024, 512], P(('rhombus', 'tile'))
- coarse_out: bfloat16 [642, 512], replicated
The draws below stay inside these ranges and needn't reach their ends.
Inputs may be any that keep to these rules, and one draw needn't show every extreme that they name: `fine_parent`: in tile t of a group, an entry p < 32 names a middle slot of the same tile, 32 <= p < 64 a slot of tile t - 1, 64 <= p a slot of tile t + 1; tile 0 never names the tile before and the last tile of a group never names the tile after. `edge_target`: in each tile the live slots come first and name a fine row of that tile; the remaining slots hold 512. Each tile has at least 1536 live slots, and some tile has all 3072 slots live.
All inputs are finite; a program needn't handle non-finite values.
Results may differ from the reference program's by a relative error of at most 0.013.
Values may be sent and summed in bfloat16 or wider, within the bound.
A program may use at most 64 MiB of HBM per device.

```python
import jax
import jax.numpy as jnp
from jax import lax

D = 512
HIDDEN_SIZE = 512
FINE_DEV = 512
MID_DEV = 32
HALO = 128
EDGES_DEV = 3072
COARSE = 642
GROUPS = 4
TILES = 8
FINE = 16384
MIDS = 1024


def draw_fine_parent(key, part):
    first_key, second_key = jax.random.split(jax.random.fold_in(key, 11))
    total = GROUPS * TILES * FINE_DEV
    side = jax.random.randint(first_key, (total,), 0, 8)
    within = jax.random.randint(second_key, (total,), 0, MID_DEV)
    tile_of = jnp.arange(total, dtype=jnp.int32) // FINE_DEV % TILES
    before = (side == 0) & (tile_of > 0)
    after = (side == 1) & (tile_of < TILES - 1)
    return jnp.where(before, within + MID_DEV, jnp.where(after, within + 2 * MID_DEV, within)).astype(jnp.int32)


def draw_mid_parent(key, part):
    near_key, far_key, pick_key = jax.random.split(jax.random.fold_in(key, 37), 3)
    blocks = GROUPS * TILES
    total = blocks * MID_DEV
    block_of = jnp.arange(total, dtype=jnp.int32) // MID_DEV
    start = block_of * COARSE // blocks
    offset = jax.random.randint(near_key, (total,), 0, 3)
    nearby = (start + offset) % COARSE
    anywhere = jax.random.randint(far_key, (total,), 0, COARSE)
    pick = jax.random.randint(pick_key, (total,), 0, 4)
    return jnp.where(pick == 0, anywhere, nearby).astype(jnp.int32)


def draw_edge_target(key, part):
    live_key, full_key, target_key = jax.random.split(jax.random.fold_in(key, 23), 3)
    blocks = GROUPS * TILES
    live = jax.random.randint(live_key, (blocks,), EDGES_DEV // 2, EDGES_DEV + 1)
    fullest = jax.random.randint(full_key, (), 0, blocks)
    live = jnp.where(jnp.arange(blocks, dtype=jnp.int32) == fullest, EDGES_DEV, live)
    slot_ids = jnp.arange(EDGES_DEV, dtype=jnp.int32)
    target = jax.random.randint(target_key, (blocks, EDGES_DEV), 0, FINE_DEV)
    marked = jnp.where(slot_ids[None, :] < live[:, None], target, FINE_DEV)
    return marked.reshape(blocks * EDGES_DEV).astype(jnp.int32)


def flat_map(key, marker, row_count, column_count, factor):
    widest = max(row_count, column_count)
    noise_key, sign_key = jax.random.split(jax.random.fold_in(key, marker))
    noise_draw = jnp.clip(jax.random.normal(noise_key, (widest, widest), jnp.float32), -4.0, 4.0)
    spread = 0.4
    skewed = (noise_draw - noise_draw.T) / jnp.sqrt(2.0 * widest)
    square = jnp.eye(widest, dtype=jnp.float32) + spread * skewed
    sign_flip = (2 * jax.random.randint(sign_key, (widest,), 0, 2) - 1).astype(jnp.float32)
    return (factor * square * sign_flip[None, :])[:row_count, :column_count]


def draw_w_child(key, part):
    return flat_map(key, 51, D, D, 1.0).astype(jnp.bfloat16)


def draw_mid_w2(key, part):
    return flat_map(key, 53, D, HIDDEN_SIZE, 0.5).astype(jnp.bfloat16)


def draw_w_coarse(key, part):
    return flat_map(key, 57, D, D, 1.0).astype(jnp.bfloat16)


def draw_coarse_w2(key, part):
    return flat_map(key, 59, D, HIDDEN_SIZE, 0.5).astype(jnp.bfloat16)


def draw_edge_w_src(key, part):
    return flat_map(key, 61, D, HIDDEN_SIZE, 1.0).astype(jnp.bfloat16)


def set_ends(drawn, key, smallest, top_value):
    shape = drawn.shape
    spot = [jax.random.randint(jax.random.fold_in(key, axis), (), 0, shape[axis]) for axis in range(len(shape))]
    drawn = drawn.at[tuple(spot)].set(smallest)
    longest = shape.index(max(shape))
    spot[longest] = (spot[longest] + 1) % shape[longest]
    return drawn.at[tuple(spot)].set(top_value)


def block_scale(own_key, shape, pieces, least, largest):
    level = 1.0
    for position, parts in pieces:
        steps = jax.random.uniform(jax.random.fold_in(jax.random.fold_in(own_key, 6), position), (parts,), jnp.float32, least / len(pieces), largest / len(pieces))
        level = level * jnp.repeat(jnp.exp(steps), shape[position] // parts).reshape((-1,) + (1,) * (len(shape) - 1 - position))
    return level


def normal_values(stream_key, dims, width, most, cuts=(), kind=jnp.bfloat16):
    values = jax.random.normal(stream_key, dims, jnp.float32) * width
    if len(cuts) > 0:
        values = block_scale(stream_key, dims, cuts, -0.22, 0.18) * values
    return jnp.clip(values, min=-most, max=most).astype(kind)


def setup_inputs(seed: int = 0) -> dict:
    splits = jax.random.split(jax.random.key(seed), 25)
    fine_latent = normal_values(splits[0], (FINE, D), 1.0, 6.0, ((0, 32),))
    mid_latent = normal_values(splits[1], (MIDS, D), 1.0, 6.0, ((0, 32),))
    coarse_latent = normal_values(splits[2], (COARSE, D), 1.0, 6.0)
    fine_parent = draw_fine_parent(jax.random.fold_in(splits[24], 71), 0)
    mid_parent = draw_mid_parent(jax.random.fold_in(splits[24], 71), 0)
    halo_rows = set_ends(jax.random.randint(splits[5], (FINE // 2,), 0, FINE_DEV), jax.random.fold_in(splits[5], 1), 0, FINE_DEV - 1).astype(jnp.int32)
    edge_source = set_ends(jax.random.randint(splits[6], (FINE * 6,), 0, FINE_DEV + 2 * HALO), jax.random.fold_in(splits[6], 1), 0, (FINE_DEV + 2 * HALO) - 1).astype(jnp.int32)
    edge_target = draw_edge_target(jax.random.fold_in(splits[24], 71), 0)
    w_child = draw_w_child(jax.random.fold_in(splits[24], 71), 0)
    mid_w1 = normal_values(splits[9], (D, HIDDEN_SIZE), D ** -0.5, 0.25)
    mid_w2 = draw_mid_w2(jax.random.fold_in(splits[24], 71), 0)
    mid_w3 = normal_values(splits[11], (HIDDEN_SIZE, D), HIDDEN_SIZE ** -0.5, 0.25)
    w_coarse = draw_w_coarse(jax.random.fold_in(splits[24], 71), 0)
    coarse_w1 = normal_values(splits[13], (D, HIDDEN_SIZE), D ** -0.5, 0.25)
    coarse_w2 = draw_coarse_w2(jax.random.fold_in(splits[24], 71), 0)
    coarse_w3 = normal_values(splits[15], (HIDDEN_SIZE, D), HIDDEN_SIZE ** -0.5, 0.25)
    w_descend = normal_values(splits[16], (D, D), D ** -0.5, 0.25)
    w_fine = normal_values(splits[17], (D, D), D ** -0.5, 0.25)
    edge_w_src = draw_edge_w_src(jax.random.fold_in(splits[24], 71), 0)
    edge_w_dst = normal_values(splits[19], (D, HIDDEN_SIZE), D ** -0.5, 0.25)
    edge_w2 = normal_values(splits[20], (HIDDEN_SIZE, D), HIDDEN_SIZE ** -0.5, 0.25)
    node_w1 = normal_values(splits[21], (D, HIDDEN_SIZE), D ** -0.5, 0.25)
    node_w2 = normal_values(splits[22], (D, HIDDEN_SIZE), (4 * D) ** -0.5, 0.125)
    node_w3 = normal_values(splits[23], (HIDDEN_SIZE, D), HIDDEN_SIZE ** -0.5, 0.25)
    return dict(fine_latent=fine_latent, mid_latent=mid_latent, coarse_latent=coarse_latent, fine_parent=fine_parent, mid_parent=mid_parent, halo_rows=halo_rows, edge_source=edge_source, edge_target=edge_target, w_child=w_child, mid_w1=mid_w1, mid_w2=mid_w2, mid_w3=mid_w3, w_coarse=w_coarse, coarse_w1=coarse_w1, coarse_w2=coarse_w2, coarse_w3=coarse_w3, w_descend=w_descend, w_fine=w_fine, edge_w_src=edge_w_src, edge_w_dst=edge_w_dst, edge_w2=edge_w2, node_w1=node_w1, node_w2=node_w2, node_w3=node_w3)


EPSILON = 1e-05

def product(left, right):
    return jnp.dot(left, right, preferred_element_type=jnp.float32)

def normed(values):
    return values / jnp.sqrt(lax.optimization_barrier(jnp.mean(values * values, axis=-1, keepdims=True)) + EPSILON)

def node_update(latent, incoming, first, second, third):
    hidden = jax.nn.silu(product(latent, first) + product(incoming, second)).astype(jnp.bfloat16)
    return (latent.astype(jnp.float32) + normed(product(hidden, third))).astype(jnp.bfloat16)

def edge_update(node_table, lifted, source, target, edge_w_src, edge_w_dst, edge_w2, node_w1, node_w2, node_w3):
    fine_count = lifted.shape[0]
    sender = product(node_table, edge_w_src).astype(jnp.bfloat16)
    receiver = product(lifted, edge_w_dst).astype(jnp.bfloat16)
    receiver = jnp.concatenate([receiver, jnp.zeros((1, receiver.shape[1]), jnp.bfloat16)], axis=0)
    edge_sum = jnp.take(sender, source, axis=0).astype(jnp.float32) + jnp.take(receiver, target, axis=0).astype(jnp.float32)
    edge_hidden = jax.nn.silu(edge_sum).astype(jnp.bfloat16)
    message = product(edge_hidden, edge_w2)
    aggregate = jax.ops.segment_sum(message, target, num_segments=fine_count + 1)[:fine_count]
    return node_update(lifted, aggregate.astype(jnp.bfloat16), node_w1, node_w2, node_w3)

def take_rows(node_block, row_ids):
    return jnp.take(node_block, row_ids, axis=0)

def reference(fine_latent, mid_latent, coarse_latent, fine_parent, mid_parent, halo_rows, edge_source, edge_target, w_child, mid_w1, mid_w2, mid_w3, w_coarse, coarse_w1, coarse_w2, coarse_w3, w_descend, w_fine, edge_w_src, edge_w_dst, edge_w2, node_w1, node_w2, node_w3):
    blocks = GROUPS * TILES
    fine_block = (jnp.arange(blocks * FINE_DEV, dtype=jnp.int32) // FINE_DEV).astype(jnp.int32)
    parent_side = (fine_parent // MID_DEV).astype(jnp.int32)
    offset = jnp.where(parent_side == 1, -1, jnp.where(parent_side == 2, 1, 0)).astype(jnp.int32)
    parent_index = ((fine_block + offset) * MID_DEV + fine_parent % MID_DEV).astype(jnp.int32)
    child_msg = product(fine_latent, w_child).astype(jnp.bfloat16)
    mid_in = jax.ops.segment_sum(child_msg.astype(jnp.float32), parent_index, num_segments=blocks * MID_DEV)
    mid_up = node_update(mid_latent, mid_in.astype(jnp.bfloat16), mid_w1, mid_w2, mid_w3)
    mid_msg = product(mid_up, w_coarse).astype(jnp.bfloat16)
    coarse_in = jax.ops.segment_sum(mid_msg.astype(jnp.float32), mid_parent, num_segments=COARSE)
    coarse_out = node_update(coarse_latent, coarse_in.astype(jnp.bfloat16), coarse_w1, coarse_w2, coarse_w3)
    down_coarse = product(coarse_out, w_descend).astype(jnp.bfloat16)
    mid_out = (mid_up.astype(jnp.float32) + jnp.take(down_coarse, mid_parent, axis=0).astype(jnp.float32)).astype(jnp.bfloat16)
    fine_down = product(mid_out, w_fine).astype(jnp.bfloat16)
    lifted = (fine_latent.astype(jnp.float32) + jnp.take(fine_down, parent_index, axis=0).astype(jnp.float32)).astype(jnp.bfloat16)
    features = lifted.shape[1]
    lifted_blocks = lifted.reshape(GROUPS, TILES, FINE_DEV, features)
    chosen = halo_rows.reshape(GROUPS, TILES, 2 * HALO)
    boundary = jax.vmap(jax.vmap(take_rows))(lifted_blocks, chosen)
    empty = jnp.zeros((GROUPS, 1, HALO, features), jnp.bfloat16)
    from_before = jnp.concatenate([empty, boundary[:, :-1, HALO:]], axis=1)
    from_after = jnp.concatenate([boundary[:, 1:, :HALO], empty], axis=1)
    node_table = jnp.concatenate([lifted_blocks, from_before, from_after], axis=2).reshape(blocks, FINE_DEV + 2 * HALO, features)

    def one_block(packed):
        return edge_update(packed[0], packed[1], packed[2], packed[3], edge_w_src, edge_w_dst, edge_w2, node_w1, node_w2, node_w3)
    fine_out = lax.map(one_block, (node_table, lifted_blocks.reshape(blocks, FINE_DEV, features), edge_source.reshape(blocks, EDGES_DEV), edge_target.reshape(blocks, EDGES_DEV)))
    return (fine_out.reshape(blocks * FINE_DEV, features), mid_out, coarse_out)
```

```python
import jax
import jax.numpy as jnp
from jax import lax
from jax.experimental import pallas as pl
from jax.experimental.pallas import tpu as pltpu
from jax.sharding import PartitionSpec as P

MESH = pl.DeviceIdType.MESH

EPSILON = 1e-05


def product(left, right):
    return jnp.dot(left, right, preferred_element_type=jnp.float32)


def normed(values):
    return values / jnp.sqrt(jnp.mean(values * values, axis=-1, keepdims=True) + EPSILON)


def node_update(latent, incoming, first, second, third):
    hidden = jax.nn.silu(product(latent, first) + product(incoming, second)).astype(jnp.bfloat16)
    return (latent.astype(jnp.float32) + normed(product(hidden, third))).astype(jnp.bfloat16)


def selector_rows(row_ids, width):
    columns = lax.broadcasted_iota(jnp.int32, (row_ids.shape[0], width), 1)
    return (columns == row_ids[:, None]).astype(jnp.bfloat16)


def edge_update(
    node_table, lifted, source, target, edge_w_src, edge_w_dst, edge_w2, node_w1, node_w2, node_w3
):
    fine_count = lifted.shape[0]
    sender = product(node_table, edge_w_src).astype(jnp.bfloat16)
    receiver = product(lifted, edge_w_dst).astype(jnp.bfloat16)
    source_pick = selector_rows(source, node_table.shape[0])
    target_pick = selector_rows(target, fine_count)
    edge_sum = product(source_pick, sender) + product(target_pick, receiver)
    edge_hidden = jax.nn.silu(edge_sum).astype(jnp.bfloat16)
    hidden_sums = lax.dot_general(
        target_pick, edge_hidden, (((0,), (0,)), ((), ())), preferred_element_type=jnp.float32
    )
    leading = hidden_sums.astype(jnp.bfloat16)
    rest = (hidden_sums - leading.astype(jnp.float32)).astype(jnp.bfloat16)
    aggregate = product(leading, edge_w2) + product(rest, edge_w2)
    return node_update(lifted, aggregate.astype(jnp.bfloat16), node_w1, node_w2, node_w3)


def one_hot(ids, axis, shape):
    return jnp.where(lax.broadcasted_iota(jnp.int32, shape, axis) == ids, 1.0, 0.0).astype(jnp.bfloat16)


def as_columns(row, width):
    count = row.shape[1]
    column = jnp.transpose(jnp.broadcast_to(row, (128, count)))
    return jnp.concatenate([column] * (width // 128), axis=1)


def gather_kernel(
    groups,
    tiles,
    fine_ref,
    parent_ref,
    halo_ref,
    latent_ref,
    coarse_id_ref,
    child_ref,
    w1_ref,
    w2_ref,
    w3_ref,
    ups_ref,
    ids_ref,
    rim_ref,
    rim_parent_ref,
    fine_v,
    child_v,
    w1_v,
    w2_v,
    w3_v,
    sums_v,
    beside_v,
    picked_v,
    picked_parent_v,
    load_sem,
    near_send,
    near_recv,
    tree_send,
    block_recv,
    id_recv,
):
    group, tile = (lax.axis_index("rhombus"), lax.axis_index("tile"))
    pairs = tiles // 2
    pair, core = (tile // 2, tile % 2)
    mids = latent_ref.shape[0]
    rims = halo_ref.shape[1] // 2
    fines = fine_ref.shape[0]

    loads = [
        pltpu.make_async_copy(src, dst, load_sem.at[i])
        for i, (src, dst) in enumerate(
            [(fine_ref, fine_v), (child_ref, child_v), (w1_ref, w1_v), (w2_ref, w2_v), (w3_ref, w3_v)]
        )
    ]
    for load in loads:
        load.start()

    def at(group_id, pair_id, core_id):
        return (group_id, pair_id * 2 + core_id)

    columns = [at((group + k) % groups, pair, core) for k in range(1, groups)]
    if pairs == 4:
        across, along = (pair + 1 - 2 * (pair % 2), (pair + 2) % 4)
        corner = (across + 2) % 4
        level = [across, along]
    else:
        level = [(pair + k) % pairs for k in range(1, pairs)]
    row_peers = [at(group, other, core) for other in level]
    partner = at(group, pair, 1 - core)
    peers = columns + row_peers + [partner]

    barrier = pltpu.get_barrier_semaphore()
    for peer in peers:
        pl.semaphore_signal(barrier, inc=1, device_id=peer, device_id_type=MESH)

    @pl.when(tile > 0)
    def _():
        pl.semaphore_signal(barrier, inc=1, device_id=(group, tile - 1), device_id_type=MESH)

    @pl.when(tile < tiles - 1)
    def _():
        pl.semaphore_signal(barrier, inc=1, device_id=(group, tile + 1), device_id_type=MESH)

    me = group * tiles + tile
    ids_ref[me] = coarse_id_ref[...]
    loads[0].wait()
    fine = fine_v[...]
    parents = parent_ref[...]
    picker = one_hot(parents, 0, (3 * mids, fines))
    sums_v[...] = product(picker, fine)
    pl.semaphore_wait(barrier, len(peers) + 1 + (tile + tiles - 1) // tiles - (tile + 1) // tiles)

    def near(index, source, target, device):
        return pltpu.make_async_remote_copy(
            src_ref=source,
            dst_ref=target,
            send_sem=near_send.at[index],
            recv_sem=near_recv.at[index],
            device_id=device,
            device_id_type=MESH,
        )

    before, after = ((group, tile - 1), (group, tile + 1))
    to_before = [
        near(0, sums_v.at[pl.ds(mids, mids)], beside_v.at[0], before),
        near(1, picked_v.at[pl.ds(0, rims)], rim_ref.at[pl.ds(rims, rims)], before),
        near(2, picked_parent_v.at[0], rim_parent_ref.at[1], before),
    ]
    to_after = [
        near(3, sums_v.at[pl.ds(2 * mids, mids)], beside_v.at[1], after),
        near(4, picked_v.at[pl.ds(rims, rims)], rim_ref.at[pl.ds(0, rims)], after),
        near(5, picked_parent_v.at[1], rim_parent_ref.at[0], after),
    ]

    @pl.when(tile > 0)
    def _():
        to_before[0].start()

    @pl.when(tile < tiles - 1)
    def _():
        to_after[0].start()

    halo = halo_ref[...]
    picked_v[...] = product(one_hot(as_columns(halo, fines), 1, (2 * rims, fines)), fine).astype(jnp.bfloat16)
    side = parents // mids
    shift = jnp.where(side == 1, -1, jnp.where(side == 2, 1, 0))
    global_parents = (me + shift) * mids + parents % mids
    parent_column = jnp.transpose(jnp.broadcast_to(global_parents, (128, fines)))
    for half in range(2):
        hit = lax.broadcasted_iota(jnp.int32, (fines, rims), 0) == halo[:, half * rims : (half + 1) * rims]
        spread = jnp.concatenate([parent_column] * (rims // 128), axis=1)
        picked_parent_v[half] = jnp.sum(jnp.where(hit, spread, 0), axis=0, keepdims=True)

    @pl.when(tile > 0)
    def _():
        to_before[1].start()
        to_before[2].start()

    @pl.when(tile < tiles - 1)
    def _():
        to_after[1].start()
        to_after[2].start()

    for load in loads[1:]:
        load.wait()
    kept = product(latent_ref[...], w1_v[...])

    @pl.when(tile > 0)
    def _():
        to_after[0].wait_recv()

    @pl.when(tile == 0)
    def _():
        beside_v[1] = jnp.zeros_like(beside_v[1])
        rim_ref[pl.ds(0, rims)] = jnp.zeros((rims, rim_ref.shape[1]), rim_ref.dtype)
        rim_parent_ref[0] = jnp.full(rim_parent_ref.shape[1:], -1, jnp.int32)

    @pl.when(tile < tiles - 1)
    def _():
        to_before[0].wait_recv()

    @pl.when(tile == tiles - 1)
    def _():
        beside_v[0] = jnp.zeros_like(beside_v[0])
        rim_ref[pl.ds(rims, rims)] = jnp.zeros((rims, rim_ref.shape[1]), rim_ref.dtype)
        rim_parent_ref[1] = jnp.full(rim_parent_ref.shape[1:], -1, jnp.int32)

    total = sums_v[pl.ds(0, mids)] + beside_v[0] + beside_v[1]
    leading = total.astype(jnp.bfloat16)
    rest = (total - leading.astype(jnp.float32)).astype(jnp.bfloat16)
    mid_in = (product(leading, child_v[...]) + product(rest, child_v[...])).astype(jnp.bfloat16)
    hidden = jax.nn.silu(kept + product(mid_in, w2_v[...])).astype(jnp.bfloat16)
    mid_up = latent_ref[...].astype(jnp.float32) + normed(product(hidden, w3_v[...]))
    ups_ref[me] = mid_up.astype(jnp.bfloat16)

    started = []

    def copies(slot, index, device):
        return [
            pltpu.make_async_remote_copy(
                src_ref=held.at[slot],
                dst_ref=held.at[slot],
                send_sem=tree_send.at[kind, index],
                recv_sem=sems.at[slot],
                device_id=device,
                device_id_type=MESH,
            )
            for kind, (held, sems) in enumerate([(ups_ref, block_recv), (ids_ref, id_recv)])
        ]

    def send(slot, devices):
        for device in devices:
            for copy in copies(slot, len(started) // 2, device):
                copy.start()
                started.append(copy)

    def arrive(slot):
        for copy in copies(slot, 0, partner):
            copy.wait_recv()

    def slot_of(k, pair_id, core_id):
        return (group + k) % groups * tiles + pair_id * 2 + core_id

    order = [0] + sorted(range(1, groups), key=lambda k: min(k, groups - k))
    send(me, columns + row_peers + [partner])
    for k in order:
        if k > 0:
            slot = slot_of(k, pair, core)
            arrive(slot)
            send(slot, row_peers + [partner])
    for n, k in enumerate(order):
        for place, other in enumerate(level):
            slot = slot_of(k, other, core)
            arrive(slot)
            onward = [partner]
            if pairs == 4 and n % 2 == place:
                onward = [at(group, level[1 - place], core), partner]
            send(slot, onward)
    if pairs == 4:
        for k in order:
            slot = slot_of(k, corner, core)
            arrive(slot)
            send(slot, [partner])
    for k in order:
        for other in range(pairs):
            arrive(slot_of(k, other, 1 - core))

    @pl.when(tile > 0)
    def _():
        for copy in to_after[1:]:
            copy.wait_recv()
        for copy in to_before:
            copy.wait_send()

    @pl.when(tile < tiles - 1)
    def _():
        for copy in to_before[1:]:
            copy.wait_recv()
        for copy in to_after:
            copy.wait_send()

    for copy in started:
        copy.wait_send()


def gathered(fine_latent, mid_latent, fine_parent, mid_parent, halo_rows, w_child, mid_w1, mid_w2, mid_w3):
    groups, tiles = (lax.axis_size("rhombus"), lax.axis_size("tile"))
    devices = groups * tiles
    mids, features = mid_latent.shape
    halos = halo_rows.shape[0]
    rims = halos // 2
    width = -(-mids // 128) * 128
    coarse_ids = jnp.pad(mid_parent[None, :], ((0, 0), (0, width - mids)))
    pairs = tiles // 2
    level = 2 if pairs == 4 else pairs - 1
    sends = groups + level + (groups - 1) * (level + 1) + groups * level
    sends += 2 * groups if pairs == 4 else 0
    bf16, f32, i32 = (jnp.bfloat16, jnp.float32, jnp.int32)
    vmem = pl.BlockSpec(memory_space=pltpu.VMEM)
    hbm = pl.BlockSpec(memory_space=pl.ANY)
    square = pltpu.VMEM((features, features), bf16)
    return pl.pallas_call(
        lambda *refs: gather_kernel(groups, tiles, *refs),
        out_shape=(
            jax.ShapeDtypeStruct((devices, mids, features), bf16),
            jax.ShapeDtypeStruct((devices, 1, width), i32),
            jax.ShapeDtypeStruct((halos, features), bf16),
            jax.ShapeDtypeStruct((2, 1, rims), i32),
        ),
        in_specs=[hbm, vmem, vmem, vmem, vmem, hbm, hbm, hbm, hbm],
        out_specs=(vmem, vmem, vmem, vmem),
        scratch_shapes=[
            pltpu.VMEM(fine_latent.shape, bf16),
            square,
            square,
            square,
            square,
            pltpu.VMEM((3 * mids, features), f32),
            pltpu.VMEM((2, mids, features), f32),
            pltpu.VMEM((halos, features), bf16),
            pltpu.VMEM((2, 1, rims), i32),
            pltpu.SemaphoreType.DMA((5,)),
            pltpu.SemaphoreType.DMA((6,)),
            pltpu.SemaphoreType.DMA((6,)),
            pltpu.SemaphoreType.DMA((2, sends)),
            pltpu.SemaphoreType.DMA((devices,)),
            pltpu.SemaphoreType.DMA((devices,)),
        ],
        compiler_params=pltpu.CompilerParams(collective_id=0, has_side_effects=True),
        name="gather_mids",
    )(
        fine_latent,
        fine_parent[None, :],
        halo_rows[None, :],
        mid_latent,
        coarse_ids,
        w_child,
        mid_w1,
        mid_w2,
        mid_w3,
    )


def on_device(
    fine_latent,
    mid_latent,
    coarse_latent,
    fine_parent,
    mid_parent,
    halo_rows,
    edge_source,
    edge_target,
    w_child,
    mid_w1,
    mid_w2,
    mid_w3,
    w_coarse,
    coarse_w1,
    coarse_w2,
    coarse_w3,
    w_descend,
    w_fine,
    edge_w_src,
    edge_w_dst,
    edge_w2,
    node_w1,
    node_w2,
    node_w3,
):
    mid_count = mid_latent.shape[0]
    coarse_count = coarse_latent.shape[0]
    rim_count = halo_rows.shape[0] // 2
    tiles = lax.axis_size("tile")
    me = lax.axis_index("rhombus") * tiles + lax.axis_index("tile")
    ups, ids, rim, rim_parent = gathered(
        fine_latent, mid_latent, fine_parent, mid_parent, halo_rows, w_child, mid_w1, mid_w2, mid_w3
    )
    mid_all = ups.reshape(-1, ups.shape[-1])
    id_all = ids[:, 0, :mid_count].reshape(-1)
    mid_msg = product(mid_all, w_coarse).astype(jnp.bfloat16)
    coarse_ids = lax.broadcasted_iota(jnp.int32, (coarse_count, id_all.shape[0]), 0)
    selector = (coarse_ids == id_all[None, :]).astype(jnp.bfloat16)
    coarse_in = product(selector, mid_msg).astype(jnp.bfloat16)
    coarse_out = node_update(coarse_latent, coarse_in, coarse_w1, coarse_w2, coarse_w3)
    reach = min(5 * mid_count, id_all.shape[0])
    low = jnp.clip((me - 2) * mid_count, 0, id_all.shape[0] - reach)
    near_up = lax.dynamic_slice_in_dim(mid_all, low, reach, 0)
    near_id = lax.dynamic_slice_in_dim(id_all, low, reach, 0)
    picked = product(selector_rows(near_id, coarse_count), coarse_out).astype(jnp.bfloat16)
    down = product(picked, w_descend).astype(jnp.bfloat16)
    near_out = (near_up.astype(jnp.float32) + down.astype(jnp.float32)).astype(jnp.bfloat16)
    mid_out = lax.dynamic_slice_in_dim(near_out, me * mid_count - low, mid_count, 0)
    fine_down = product(near_out, w_fine).astype(jnp.bfloat16)
    side = fine_parent // mid_count
    shift = jnp.where(side == 1, -1, jnp.where(side == 2, 1, 0))
    own_parent = (me + shift) * mid_count + fine_parent % mid_count
    table_parent = jnp.concatenate([own_parent, rim_parent.reshape(-1)]) - low
    table_parent = jnp.where(
        jnp.concatenate([own_parent, rim_parent.reshape(-1)]) < 0, -1, table_parent
    )
    raised = product(selector_rows(table_parent, reach), fine_down)
    node_table = (jnp.concatenate([fine_latent, rim], axis=0).astype(jnp.float32) + raised).astype(jnp.bfloat16)
    lifted = node_table[: fine_latent.shape[0]]
    fine_out = edge_update(
        node_table,
        lifted,
        edge_source,
        edge_target,
        edge_w_src,
        edge_w_dst,
        edge_w2,
        node_w1,
        node_w2,
        node_w3,
    )
    return (fine_out, mid_out, coarse_out)


def solution(mesh):
    placed = (
        P(("rhombus", "tile"), None),
        P(("rhombus", "tile"), None),
        P(),
        P(("rhombus", "tile")),
        P(("rhombus", "tile")),
        P(("rhombus", "tile")),
        P(("rhombus", "tile")),
        P(("rhombus", "tile")),
        P(),
        P(),
        P(),
        P(),
        P(),
        P(),
        P(),
        P(),
        P(),
        P(),
        P(),
        P(),
        P(),
        P(),
        P(),
        P(),
    )
    return jax.shard_map(
        on_device,
        mesh=mesh,
        in_specs=placed,
        out_specs=(P(("rhombus", "tile"), None), P(("rhombus", "tile"), None), P()),
        check_vma=False,
    )
```

```python
import jax
import jax.numpy as jnp
from jax import lax
from jax.experimental import pallas as pl
from jax.experimental.pallas import tpu as pltpu
from jax.sharding import PartitionSpec as P

MESH = pl.DeviceIdType.MESH

EPSILON = 1e-05


def product(left, right):
    return jnp.dot(left, right, preferred_element_type=jnp.float32)


def normed(values):
    return values / jnp.sqrt(jnp.mean(values * values, axis=-1, keepdims=True) + EPSILON)


def one_hot(ids, axis, shape):
    return jnp.where(lax.broadcasted_iota(jnp.int32, shape, axis) == ids, 1.0, 0.0).astype(jnp.bfloat16)


def as_columns(row, width):
    count = row.shape[1]
    column = jnp.transpose(jnp.broadcast_to(row, (128, count)))
    return jnp.concatenate([column] * (width // 128), axis=1)


def gather_kernel(
    groups,
    tiles,
    fine_ref,
    parent_ref,
    halo_ref,
    latent_ref,
    coarse_id_ref,
    child_ref,
    w1_ref,
    w2_ref,
    w3_ref,
    ups_ref,
    ids_ref,
    rim_ref,
    rim_parent_ref,
    fine_v,
    child_v,
    w1_v,
    w2_v,
    w3_v,
    sums_v,
    beside_v,
    picked_v,
    picked_parent_v,
    load_sem,
    near_send,
    near_recv,
    tree_send,
    block_recv,
    id_recv,
):
    group, tile = (lax.axis_index("rhombus"), lax.axis_index("tile"))
    pairs = tiles // 2
    pair, core = (tile // 2, tile % 2)
    mids = latent_ref.shape[0]
    rims = halo_ref.shape[1] // 2
    fines = fine_ref.shape[0]

    loads = [
        pltpu.make_async_copy(src, dst, load_sem.at[i])
        for i, (src, dst) in enumerate(
            [(fine_ref, fine_v), (child_ref, child_v), (w1_ref, w1_v), (w2_ref, w2_v), (w3_ref, w3_v)]
        )
    ]
    for load in loads:
        load.start()

    def at(group_id, pair_id, core_id):
        return (group_id, pair_id * 2 + core_id)

    columns = [at((group + k) % groups, pair, core) for k in range(1, groups)]
    if pairs == 4:
        across, along = (pair + 1 - 2 * (pair % 2), (pair + 2) % 4)
        corner = (across + 2) % 4
        level = [across, along]
    else:
        level = [(pair + k) % pairs for k in range(1, pairs)]
    row_peers = [at(group, other, core) for other in level]
    partner = at(group, pair, 1 - core)
    peers = columns + row_peers + [partner]

    barrier = pltpu.get_barrier_semaphore()
    for peer in peers:
        pl.semaphore_signal(barrier, inc=1, device_id=peer, device_id_type=MESH)

    @pl.when(tile > 0)
    def _():
        pl.semaphore_signal(barrier, inc=1, device_id=(group, tile - 1), device_id_type=MESH)

    @pl.when(tile < tiles - 1)
    def _():
        pl.semaphore_signal(barrier, inc=1, device_id=(group, tile + 1), device_id_type=MESH)

    me = group * tiles + tile
    ids_ref[me] = coarse_id_ref[...]
    loads[0].wait()
    fine = fine_v[...]
    parents = parent_ref[...]
    picker = one_hot(parents, 0, (3 * mids, fines))
    sums_v[...] = product(picker, fine)
    pl.semaphore_wait(barrier, len(peers) + 1 + (tile + tiles - 1) // tiles - (tile + 1) // tiles)

    def near(index, source, target, device):
        return pltpu.make_async_remote_copy(
            src_ref=source,
            dst_ref=target,
            send_sem=near_send.at[index],
            recv_sem=near_recv.at[index],
            device_id=device,
            device_id_type=MESH,
        )

    before, after = ((group, tile - 1), (group, tile + 1))
    to_before = [
        near(0, sums_v.at[pl.ds(mids, mids)], beside_v.at[0], before),
        near(1, picked_v.at[pl.ds(0, rims)], rim_ref.at[pl.ds(rims, rims)], before),
        near(2, picked_parent_v.at[0], rim_parent_ref.at[1], before),
    ]
    to_after = [
        near(3, sums_v.at[pl.ds(2 * mids, mids)], beside_v.at[1], after),
        near(4, picked_v.at[pl.ds(rims, rims)], rim_ref.at[pl.ds(0, rims)], after),
        near(5, picked_parent_v.at[1], rim_parent_ref.at[0], after),
    ]

    @pl.when(tile > 0)
    def _():
        to_before[0].start()

    @pl.when(tile < tiles - 1)
    def _():
        to_after[0].start()

    halo = halo_ref[...]
    picked_v[...] = product(one_hot(as_columns(halo, fines), 1, (2 * rims, fines)), fine).astype(jnp.bfloat16)
    side = parents // mids
    shift = jnp.where(side == 1, -1, jnp.where(side == 2, 1, 0))
    global_parents = (me + shift) * mids + parents % mids
    parent_column = jnp.transpose(jnp.broadcast_to(global_parents, (128, fines)))
    for half in range(2):
        hit = lax.broadcasted_iota(jnp.int32, (fines, rims), 0) == halo[:, half * rims : (half + 1) * rims]
        spread = jnp.concatenate([parent_column] * (rims // 128), axis=1)
        picked_parent_v[half] = jnp.sum(jnp.where(hit, spread, 0), axis=0, keepdims=True)

    @pl.when(tile > 0)
    def _():
        to_before[1].start()
        to_before[2].start()

    @pl.when(tile < tiles - 1)
    def _():
        to_after[1].start()
        to_after[2].start()

    for load in loads[1:]:
        load.wait()
    kept = product(latent_ref[...], w1_v[...])

    @pl.when(tile > 0)
    def _():
        to_after[0].wait_recv()

    @pl.when(tile == 0)
    def _():
        beside_v[1] = jnp.zeros_like(beside_v[1])
        rim_ref[pl.ds(0, rims)] = jnp.zeros((rims, rim_ref.shape[1]), rim_ref.dtype)
        rim_parent_ref[0] = jnp.full(rim_parent_ref.shape[1:], -1, jnp.int32)

    @pl.when(tile < tiles - 1)
    def _():
        to_before[0].wait_recv()

    @pl.when(tile == tiles - 1)
    def _():
        beside_v[0] = jnp.zeros_like(beside_v[0])
        rim_ref[pl.ds(rims, rims)] = jnp.zeros((rims, rim_ref.shape[1]), rim_ref.dtype)
        rim_parent_ref[1] = jnp.full(rim_parent_ref.shape[1:], -1, jnp.int32)

    total = sums_v[pl.ds(0, mids)] + beside_v[0] + beside_v[1]
    leading = total.astype(jnp.bfloat16)
    rest = (total - leading.astype(jnp.float32)).astype(jnp.bfloat16)
    mid_in = (product(leading, child_v[...]) + product(rest, child_v[...])).astype(jnp.bfloat16)
    hidden = jax.nn.silu(kept + product(mid_in, w2_v[...])).astype(jnp.bfloat16)
    mid_up = latent_ref[...].astype(jnp.float32) + normed(product(hidden, w3_v[...]))
    ups_ref[me] = mid_up.astype(jnp.bfloat16)

    started = []

    def copies(slot, index, device):
        return [
            pltpu.make_async_remote_copy(
                src_ref=held.at[slot],
                dst_ref=held.at[slot],
                send_sem=tree_send.at[kind, index],
                recv_sem=sems.at[slot],
                device_id=device,
                device_id_type=MESH,
            )
            for kind, (held, sems) in enumerate([(ups_ref, block_recv), (ids_ref, id_recv)])
        ]

    def send(slot, devices):
        for device in devices:
            for copy in copies(slot, len(started) // 2, device):
                copy.start()
                started.append(copy)

    def arrive(slot):
        for copy in copies(slot, 0, partner):
            copy.wait_recv()

    def slot_of(k, pair_id, core_id):
        return (group + k) % groups * tiles + pair_id * 2 + core_id

    order = [0] + sorted(range(1, groups), key=lambda k: min(k, groups - k))
    send(me, columns + row_peers + [partner])
    for k in order:
        if k > 0:
            slot = slot_of(k, pair, core)
            arrive(slot)
            send(slot, row_peers + [partner])
    for n, k in enumerate(order):
        for place, other in enumerate(level):
            slot = slot_of(k, other, core)
            arrive(slot)
            onward = [partner]
            if pairs == 4 and n % 2 == place:
                onward = [at(group, level[1 - place], core), partner]
            send(slot, onward)
    if pairs == 4:
        for k in order:
            slot = slot_of(k, corner, core)
            arrive(slot)
            send(slot, [partner])
    for k in order:
        for other in range(pairs):
            arrive(slot_of(k, other, 1 - core))

    @pl.when(tile > 0)
    def _():
        for copy in to_after[1:]:
            copy.wait_recv()
        for copy in to_before:
            copy.wait_send()

    @pl.when(tile < tiles - 1)
    def _():
        for copy in to_before[1:]:
            copy.wait_recv()
        for copy in to_after:
            copy.wait_send()

    for copy in started:
        copy.wait_send()


def gathered(fine_latent, mid_latent, fine_parent, mid_parent, halo_rows, w_child, mid_w1, mid_w2, mid_w3):
    groups, tiles = (lax.axis_size("rhombus"), lax.axis_size("tile"))
    devices = groups * tiles
    mids, features = mid_latent.shape
    halos = halo_rows.shape[0]
    rims = halos // 2
    width = -(-mids // 128) * 128
    coarse_ids = jnp.pad(mid_parent[None, :], ((0, 0), (0, width - mids)))
    pairs = tiles // 2
    level = 2 if pairs == 4 else pairs - 1
    sends = groups + level + (groups - 1) * (level + 1) + groups * level
    sends += 2 * groups if pairs == 4 else 0
    bf16, f32, i32 = (jnp.bfloat16, jnp.float32, jnp.int32)
    vmem = pl.BlockSpec(memory_space=pltpu.VMEM)
    hbm = pl.BlockSpec(memory_space=pl.ANY)
    square = pltpu.VMEM((features, features), bf16)
    return pl.pallas_call(
        lambda *refs: gather_kernel(groups, tiles, *refs),
        out_shape=(
            jax.ShapeDtypeStruct((devices, mids, features), bf16),
            jax.ShapeDtypeStruct((devices, 1, width), i32),
            jax.ShapeDtypeStruct((halos, features), bf16),
            jax.ShapeDtypeStruct((2, 1, rims), i32),
        ),
        in_specs=[hbm, vmem, vmem, vmem, vmem, hbm, hbm, hbm, hbm],
        out_specs=(vmem, vmem, vmem, vmem),
        scratch_shapes=[
            pltpu.VMEM(fine_latent.shape, bf16),
            square,
            square,
            square,
            square,
            pltpu.VMEM((3 * mids, features), f32),
            pltpu.VMEM((2, mids, features), f32),
            pltpu.VMEM((halos, features), bf16),
            pltpu.VMEM((2, 1, rims), i32),
            pltpu.SemaphoreType.DMA((5,)),
            pltpu.SemaphoreType.DMA((6,)),
            pltpu.SemaphoreType.DMA((6,)),
            pltpu.SemaphoreType.DMA((2, sends)),
            pltpu.SemaphoreType.DMA((devices,)),
            pltpu.SemaphoreType.DMA((devices,)),
        ],
        compiler_params=pltpu.CompilerParams(collective_id=0, has_side_effects=True),
        name="gather_mids",
    )(
        fine_latent,
        fine_parent[None, :],
        halo_rows[None, :],
        mid_latent,
        coarse_ids,
        w_child,
        mid_w1,
        mid_w2,
        mid_w3,
    )


def gate(values):
    return values * (0.5 + 0.5 * jnp.tanh(0.5 * values))


def tail_kernel(
    groups,
    tiles,
    ups_ref,
    ids_ref,
    rim_ref,
    rim_parent_ref,
    fine_parent_ref,
    source_ref,
    target_ref,
    coarse_ref,
    fine_ref,
    w_coarse_ref,
    c1_ref,
    c2_ref,
    c3_ref,
    descend_ref,
    w_fine_ref,
    src_w_ref,
    dst_w_ref,
    e2_ref,
    n1_ref,
    n2_ref,
    n3_ref,
    fine_out_ref,
    mid_out_ref,
    coarse_out_ref,
    fine_v,
    weights_v,
    coarse_v,
    near_v,
    down_v,
    table_v,
    sent_v,
    got_v,
    sums_v,
    load_sem,
):
    bf16, f32 = (jnp.bfloat16, jnp.float32)
    me = lax.axis_index("rhombus") * tiles + lax.axis_index("tile")
    devices, mids, features = ups_ref.shape
    fines = fine_v.shape[0]
    coarse_count = coarse_ref.shape[0]
    rims = rim_ref.shape[0] // 2
    reach = min(5, devices)
    names = [
        w_coarse_ref, c1_ref, c2_ref, c3_ref, descend_ref, w_fine_ref,
        src_w_ref, dst_w_ref, e2_ref, n1_ref, n2_ref, n3_ref,
    ]
    loads = [pltpu.make_async_copy(ref, weights_v.at[i], load_sem.at[i]) for i, ref in enumerate(names)]
    loads.insert(6, pltpu.make_async_copy(fine_ref, fine_v, load_sem.at[len(names)]))
    for load in loads:
        load.start()

    def weight(i):
        loads[i if i < 6 else i + 1].wait()
        return weights_v[i]

    mid_all = ups_ref[...].reshape(devices * mids, features)
    mid_msg = product(mid_all, weight(0)).astype(bf16)
    id_row = jnp.concatenate([ids_ref[d][:, :mids] for d in range(devices)], axis=1)
    coarse_in = product(one_hot(id_row, 0, (coarse_count, devices * mids)), mid_msg).astype(bf16)
    coarse = coarse_ref[...]
    hidden = gate(product(coarse, weight(1)) + product(coarse_in, weight(2))).astype(bf16)
    updated = (coarse.astype(f32) + normed(product(hidden, weight(3)))).astype(bf16)
    coarse_out_ref[...] = updated
    padded = coarse_v.shape[0]
    edge = coarse_count // 16 * 16
    coarse_v[edge:] = jnp.zeros((padded - edge, features), bf16)
    coarse_v[:coarse_count] = updated

    low = jnp.clip(me - 2, 0, devices - reach)
    near = near_v.shape[0]
    window = reach * mids
    spare = down_v.shape[0] - window
    near_row = jnp.concatenate(
        [ids_ref[low + d][:, :mids] for d in range(reach)] + [jnp.zeros((1, spare), jnp.int32)], axis=1
    )
    pick = one_hot(as_columns(near_row, padded)[:window], 1, (window, padded))
    picked = product(pick, coarse_v[...]).astype(bf16)
    down = product(picked, weight(4)).astype(bf16)
    near_up = ups_ref[pl.ds(low, reach)].reshape(window, features)
    near_out = (near_up.astype(f32) + down.astype(f32)).astype(bf16)
    near_v[...] = near_out.reshape(reach, mids, features)
    mid_out_ref[...] = near_v[me - low]
    down_v[:window] = product(near_out, weight(5)).astype(bf16)
    down_v[window:] = jnp.zeros((spare, features), bf16)

    parents = fine_parent_ref[...]
    side = parents // mids
    shift = jnp.where(side == 1, -1, jnp.where(side == 2, 1, 0))
    own_parent = (me + shift) * mids + parents % mids
    table_parent = jnp.concatenate([own_parent, rim_parent_ref[0], rim_parent_ref[1]], axis=1)
    table_parent = jnp.where(table_parent < 0, -1, table_parent - low * mids)
    width = down_v.shape[0]
    lift = one_hot(as_columns(table_parent, width), 1, (fines + 2 * rims, width))
    raised = product(lift, down_v[...])
    loads[6].wait()
    table_v[:fines] = (fine_v[...].astype(f32) + raised[:fines]).astype(bf16)
    table_v[fines:] = (rim_ref[...].astype(f32) + raised[fines:]).astype(bf16)

    across = (((1,), (1,)), ((), ()))

    def flipped(w, rows):
        return lax.dot_general(jnp.transpose(w), rows, across, preferred_element_type=f32).astype(bf16)

    lifted = table_v[:fines]
    sent_v[...] = flipped(weight(6), table_v[...])
    got_v[...] = flipped(weight(7), lifted)
    sums_v[...] = jnp.zeros(sums_v.shape, f32)
    edges = source_ref.shape[1]
    step = next(size for size in (1024, 512, 256, 128) if edges % size == 0)

    def block(i, carry):
        at = pl.ds(pl.multiple_of(i * step, step), step)
        source_pick = one_hot(source_ref[:, at], 0, (fines + 2 * rims, step))
        target_pick = one_hot(target_ref[:, at], 0, (fines, step))
        edge_sum = product(sent_v[...], source_pick) + product(got_v[...], target_pick)
        edge_hidden = gate(edge_sum).astype(bf16)
        sums_v[...] += lax.dot_general(target_pick, edge_hidden, across, preferred_element_type=f32)
        return carry

    lax.fori_loop(0, edges // step, block, 0)
    sums = sums_v[...]
    leading = sums.astype(bf16)
    rest = (sums - leading.astype(f32)).astype(bf16)
    e2 = weight(8)
    aggregate = (product(leading, e2) + product(rest, e2)).astype(bf16)
    hidden = gate(product(lifted, weight(9)) + product(aggregate, weight(10))).astype(bf16)
    fine_out_ref[...] = (lifted.astype(f32) + normed(product(hidden, weight(11)))).astype(bf16)


def finished(ups, ids, rim, rim_parent, fine_latent, coarse_latent, fine_parent, edge_source, edge_target, weights):
    groups, tiles = (lax.axis_size("rhombus"), lax.axis_size("tile"))
    devices, mids, features = ups.shape
    fines = fine_latent.shape[0]
    halos = rim.shape[0]
    bf16, f32 = (jnp.bfloat16, jnp.float32)
    vmem = pl.BlockSpec(memory_space=pltpu.VMEM)
    hbm = pl.BlockSpec(memory_space=pl.ANY)
    reach = min(5, devices)
    ceil = lambda n: -(-n // 128) * 128
    return pl.pallas_call(
        lambda *refs: tail_kernel(groups, tiles, *refs),
        out_shape=(
            jax.ShapeDtypeStruct(fine_latent.shape, bf16),
            jax.ShapeDtypeStruct((mids, features), bf16),
            jax.ShapeDtypeStruct(coarse_latent.shape, bf16),
        ),
        in_specs=[vmem] * 8 + [hbm] * (1 + len(weights)),
        out_specs=(vmem, vmem, vmem),
        scratch_shapes=[
            pltpu.VMEM(fine_latent.shape, bf16),
            pltpu.VMEM((len(weights), features, features), bf16),
            pltpu.VMEM((ceil(coarse_latent.shape[0]), features), bf16),
            pltpu.VMEM((reach, mids, features), bf16),
            pltpu.VMEM((ceil(reach * mids), features), bf16),
            pltpu.VMEM((fines + halos, features), bf16),
            pltpu.VMEM((features, fines + halos), bf16),
            pltpu.VMEM((features, fines), bf16),
            pltpu.VMEM((fines, features), f32),
            pltpu.SemaphoreType.DMA((len(weights) + 1,)),
        ],
        name="tail",
    )(
        ups,
        ids,
        rim,
        rim_parent,
        fine_parent[None, :],
        edge_source[None, :],
        edge_target[None, :],
        coarse_latent,
        fine_latent,
        *weights,
    )


def on_device(
    fine_latent,
    mid_latent,
    coarse_latent,
    fine_parent,
    mid_parent,
    halo_rows,
    edge_source,
    edge_target,
    w_child,
    mid_w1,
    mid_w2,
    mid_w3,
    w_coarse,
    coarse_w1,
    coarse_w2,
    coarse_w3,
    w_descend,
    w_fine,
    edge_w_src,
    edge_w_dst,
    edge_w2,
    node_w1,
    node_w2,
    node_w3,
):
    ups, ids, rim, rim_parent = gathered(
        fine_latent, mid_latent, fine_parent, mid_parent, halo_rows, w_child, mid_w1, mid_w2, mid_w3
    )
    weights = (
        w_coarse,
        coarse_w1,
        coarse_w2,
        coarse_w3,
        w_descend,
        w_fine,
        edge_w_src,
        edge_w_dst,
        edge_w2,
        node_w1,
        node_w2,
        node_w3,
    )
    return finished(
        ups, ids, rim, rim_parent, fine_latent, coarse_latent, fine_parent, edge_source, edge_target, weights
    )


def solution(mesh):
    placed = (
        P(("rhombus", "tile"), None),
        P(("rhombus", "tile"), None),
        P(),
        P(("rhombus", "tile")),
        P(("rhombus", "tile")),
        P(("rhombus", "tile")),
        P(("rhombus", "tile")),
        P(("rhombus", "tile")),
        P(),
        P(),
        P(),
        P(),
        P(),
        P(),
        P(),
        P(),
        P(),
        P(),
        P(),
        P(),
        P(),
        P(),
        P(),
        P(),
    )
    return jax.shard_map(
        on_device,
        mesh=mesh,
        in_specs=placed,
        out_specs=(P(("rhombus", "tile"), None), P(("rhombus", "tile"), None), P()),
        check_vma=False,
    )
```

```python
import jax
import jax.numpy as jnp
from jax import lax
from jax.experimental import pallas as pl
from jax.experimental.pallas import tpu as pltpu
from jax.sharding import PartitionSpec as P

MESH = pl.DeviceIdType.MESH

EPSILON = 1e-05


def product(left, right):
    return jnp.dot(left, right, preferred_element_type=jnp.float32)


def normed(values):
    return values / jnp.sqrt(jnp.mean(values * values, axis=-1, keepdims=True) + EPSILON)


def gate(values):
    return values * (0.5 + 0.5 * jnp.tanh(0.5 * values))


def one_hot(ids, axis, shape):
    return jnp.where(lax.broadcasted_iota(jnp.int32, shape, axis) == ids, 1.0, 0.0).astype(jnp.bfloat16)


def as_columns(row, width):
    count = row.shape[1]
    column = jnp.transpose(jnp.broadcast_to(row, (128, count)))
    return jnp.concatenate([column] * (width // 128), axis=1)


def sweep_kernel(
    groups,
    tiles,
    parent_ref,
    halo_ref,
    latent_ref,
    coarse_id_ref,
    source_ref,
    target_ref,
    coarse_ref,
    fine_ref,
    *rest_refs,
):
    weight_refs = rest_refs[:16]
    fine_out_ref, mid_out_ref, coarse_out_ref = rest_refs[16:19]
    ups_ref, ids_ref, rim_ref, rim_parent_ref, fine_v, weights_v = rest_refs[19:25]
    sums_v, beside_v, picked_v, picked_parent_v, kept_v, flip_v, into_v = rest_refs[25:32]
    coarse_v, down_v, table_v, sent_v, got_v, edge_v = rest_refs[32:38]
    load_sem, near_send, near_recv, tree_send, block_recv, id_recv = rest_refs[38:]
    group, tile = (lax.axis_index("rhombus"), lax.axis_index("tile"))
    pairs = tiles // 2
    pair, core = (tile // 2, tile % 2)
    mids = latent_ref.shape[0]
    rims = halo_ref.shape[1] // 2
    fines, features = fine_ref.shape

    bf16, f32 = (jnp.bfloat16, jnp.float32)
    loads = [pltpu.make_async_copy(fine_ref, fine_v, load_sem.at[len(weight_refs)])]
    loads += [pltpu.make_async_copy(ref, weights_v.at[i], load_sem.at[i]) for i, ref in enumerate(weight_refs)]
    for load in loads:
        load.start()

    def weight(i):
        loads[i + 1].wait()
        return weights_v[i]

    def at(group_id, pair_id, core_id):
        return (group_id, pair_id * 2 + core_id)

    columns = [at((group + k) % groups, pair, core) for k in range(1, groups)]
    if pairs == 4:
        across, along = (pair + 1 - 2 * (pair % 2), (pair + 2) % 4)
        corner = (across + 2) % 4
        level = [across, along]
    else:
        level = [(pair + k) % pairs for k in range(1, pairs)]
    row_peers = [at(group, other, core) for other in level]
    partner = at(group, pair, 1 - core)
    peers = columns + row_peers + [partner]

    barrier = pltpu.get_barrier_semaphore()
    for peer in peers:
        pl.semaphore_signal(barrier, inc=1, device_id=peer, device_id_type=MESH)

    @pl.when(tile > 0)
    def _():
        pl.semaphore_signal(barrier, inc=1, device_id=(group, tile - 1), device_id_type=MESH)

    @pl.when(tile < tiles - 1)
    def _():
        pl.semaphore_signal(barrier, inc=1, device_id=(group, tile + 1), device_id_type=MESH)

    me = group * tiles + tile
    halves = groups * pairs

    def place_of(group_id, pair_id, core_id):
        return core_id * halves + group_id * pairs + pair_id

    mine = place_of(group, pair, core)
    ids_ref[mine] = coarse_id_ref[...]
    loads[0].wait()
    fine = fine_v[...]
    parents = parent_ref[...]
    picker = one_hot(parents, 0, (3 * mids, fines))
    sums_v[...] = product(picker, fine)
    pl.semaphore_wait(barrier, len(peers) + 1 + (tile + tiles - 1) // tiles - (tile + 1) // tiles)

    def near(index, source, target, device):
        return pltpu.make_async_remote_copy(
            src_ref=source,
            dst_ref=target,
            send_sem=near_send.at[index],
            recv_sem=near_recv.at[index],
            device_id=device,
            device_id_type=MESH,
        )

    before, after = ((group, tile - 1), (group, tile + 1))
    to_before = [
        near(0, sums_v.at[pl.ds(mids, mids)], beside_v.at[0], before),
        near(1, picked_v.at[pl.ds(0, rims)], rim_ref.at[pl.ds(rims, rims)], before),
        near(2, picked_parent_v.at[0], rim_parent_ref.at[1], before),
    ]
    to_after = [
        near(3, sums_v.at[pl.ds(2 * mids, mids)], beside_v.at[1], after),
        near(4, picked_v.at[pl.ds(rims, rims)], rim_ref.at[pl.ds(0, rims)], after),
        near(5, picked_parent_v.at[1], rim_parent_ref.at[0], after),
    ]

    @pl.when(tile > 0)
    def _():
        to_before[0].start()

    @pl.when(tile < tiles - 1)
    def _():
        to_after[0].start()

    halo = halo_ref[...]
    picked_v[...] = product(one_hot(as_columns(halo, fines), 1, (2 * rims, fines)), fine).astype(jnp.bfloat16)
    side = parents // mids
    shift = jnp.where(side == 1, -1, jnp.where(side == 2, 1, 0))
    global_parents = (me + shift) * mids + parents % mids
    parent_column = jnp.transpose(jnp.broadcast_to(global_parents, (128, fines)))
    for half in range(2):
        hit = lax.broadcasted_iota(jnp.int32, (fines, rims), 0) == halo[:, half * rims : (half + 1) * rims]
        spread = jnp.concatenate([parent_column] * (rims // 128), axis=1)
        picked_parent_v[half] = jnp.sum(jnp.where(hit, spread, 0), axis=0, keepdims=True)

    @pl.when(tile > 0)
    def _():
        to_before[1].start()
        to_before[2].start()

    @pl.when(tile < tiles - 1)
    def _():
        to_after[1].start()
        to_after[2].start()

    child_w = weight(0)
    kept = product(latent_ref[...], weight(1))

    @pl.when(tile > 0)
    def _():
        to_after[0].wait_recv()

    @pl.when(tile == 0)
    def _():
        beside_v[1] = jnp.zeros_like(beside_v[1])
        rim_ref[pl.ds(0, rims)] = jnp.zeros((rims, rim_ref.shape[1]), rim_ref.dtype)
        rim_parent_ref[0] = jnp.full(rim_parent_ref.shape[1:], -1, jnp.int32)

    @pl.when(tile < tiles - 1)
    def _():
        to_before[0].wait_recv()

    @pl.when(tile == tiles - 1)
    def _():
        beside_v[0] = jnp.zeros_like(beside_v[0])
        rim_ref[pl.ds(rims, rims)] = jnp.zeros((rims, rim_ref.shape[1]), rim_ref.dtype)
        rim_parent_ref[1] = jnp.full(rim_parent_ref.shape[1:], -1, jnp.int32)

    total = sums_v[pl.ds(0, mids)] + beside_v[0] + beside_v[1]
    leading = total.astype(jnp.bfloat16)
    rest = (total - leading.astype(jnp.float32)).astype(jnp.bfloat16)
    mid_in = (product(leading, child_w) + product(rest, child_w)).astype(jnp.bfloat16)
    hidden = gate(kept + product(mid_in, weight(2))).astype(jnp.bfloat16)
    mid_up = latent_ref[...].astype(jnp.float32) + normed(product(hidden, weight(3)))
    ups_ref[mine] = mid_up.astype(jnp.bfloat16)

    started = []

    def copies(slot, index, device):
        return [
            pltpu.make_async_remote_copy(
                src_ref=held.at[slot],
                dst_ref=held.at[slot],
                send_sem=tree_send.at[kind, index],
                recv_sem=sems.at[slot],
                device_id=device,
                device_id_type=MESH,
            )
            for kind, (held, sems) in enumerate([(ups_ref, block_recv), (ids_ref, id_recv)])
        ]

    def send(slot, devices):
        for device in devices:
            for copy in copies(slot, len(started) // 2, device):
                copy.start()
                started.append(copy)

    def arrive(slot):
        for copy in copies(slot, 0, partner):
            copy.wait_recv()

    def slot_of(k, pair_id, core_id):
        return place_of((group + k) % groups, pair_id, core_id)

    order = [0] + sorted(range(1, groups), key=lambda k: min(k, groups - k))
    send(mine, columns + row_peers + [partner])
    coarse = coarse_ref[...]
    kept_v[...] = product(coarse, weight(4))
    flip_v[0] = jnp.transpose(weight(5))
    flip_v[1] = jnp.transpose(weight(6))
    for k in order:
        if k > 0:
            slot = slot_of(k, pair, core)
            arrive(slot)
            send(slot, row_peers + [partner])
    for n, k in enumerate(order):
        for place, other in enumerate(level):
            slot = slot_of(k, other, core)
            arrive(slot)
            onward = [partner]
            if pairs == 4 and n % 2 == place:
                onward = [at(group, level[1 - place], core), partner]
            send(slot, onward)
    if pairs == 4:
        for k in order:
            slot = slot_of(k, corner, core)
            arrive(slot)
            send(slot, [partner])
    w_coarse = weight(7)
    coarse_count = coarse.shape[0]

    def half_sum(half):
        held = pl.ds(half * halves, halves)
        mid_msg = product(ups_ref[held].reshape(halves * mids, features), w_coarse).astype(bf16)
        id_row = jnp.concatenate([ids_ref[half * halves + d][:, :mids] for d in range(halves)], axis=1)
        return product(one_hot(id_row, 0, (coarse_count, halves * mids)), mid_msg)

    into_v[...] = half_sum(core)
    for k in order:
        for other in range(pairs):
            arrive(slot_of(k, other, 1 - core))

    @pl.when(tile > 0)
    def _():
        for copy in to_after[1:]:
            copy.wait_recv()

    @pl.when(tile < tiles - 1)
    def _():
        for copy in to_before[1:]:
            copy.wait_recv()

    coarse_in = (into_v[...] + half_sum(1 - core)).astype(bf16)
    hidden = gate(kept_v[...] + product(coarse_in, weight(8))).astype(bf16)
    updated = (coarse.astype(f32) + normed(product(hidden, weight(9)))).astype(bf16)
    coarse_out_ref[...] = updated
    padded = coarse_v.shape[0]
    edge = coarse_count // 16 * 16
    coarse_v[edge:] = jnp.zeros((padded - edge, features), bf16)
    coarse_v[:coarse_count] = updated

    nearby = []
    for d in range(-2, 3):
        other = (me + d + 2 * groups * tiles) % (groups * tiles)
        other_tile = other % tiles
        nearby.append(place_of(other // tiles, other_tile // 2, other_tile % 2))
    window = len(nearby) * mids
    spare = down_v.shape[0] - window
    near_row = jnp.concatenate(
        [ids_ref[slot][:, :mids] for slot in nearby] + [jnp.zeros((1, spare), jnp.int32)], axis=1
    )
    pick = one_hot(as_columns(near_row, padded)[:window], 1, (window, padded))
    picked = product(pick, coarse_v[...]).astype(bf16)
    down = product(picked, weight(10)).astype(bf16)
    near_up = jnp.concatenate([ups_ref[slot] for slot in nearby], axis=0)
    near_out = (near_up.astype(f32) + down.astype(f32)).astype(bf16)
    mid_out_ref[...] = near_out[2 * mids : 3 * mids]
    down_v[:window] = product(near_out, weight(11)).astype(bf16)
    down_v[window:] = jnp.zeros((spare, features), bf16)

    own_parent = (2 + shift) * mids + parents % mids
    far_parent = jnp.concatenate([rim_parent_ref[0], rim_parent_ref[1]], axis=1)
    far_parent = jnp.where(far_parent < 0, -1, far_parent - (me - 2) * mids)
    table_parent = jnp.concatenate([own_parent, far_parent], axis=1)
    width = down_v.shape[0]
    lift = one_hot(as_columns(table_parent, width), 1, (fines + 2 * rims, width))
    raised = product(lift, down_v[...])
    table_v[:fines] = (fine.astype(f32) + raised[:fines]).astype(bf16)
    table_v[fines:] = (rim_ref[...].astype(f32) + raised[fines:]).astype(bf16)

    across = (((1,), (1,)), ((), ()))

    def flipped(w, rows):
        return lax.dot_general(w, rows, across, preferred_element_type=f32).astype(bf16)

    lifted = table_v[:fines]
    sent_v[...] = flipped(flip_v[0], table_v[...])
    got_v[...] = flipped(flip_v[1], lifted)
    edge_v[...] = jnp.zeros(edge_v.shape, f32)
    edges = source_ref.shape[1]
    step = next(size for size in (1024, 512, 256, 128) if edges % size == 0)

    def block(i, carry):
        at = pl.ds(pl.multiple_of(i * step, step), step)
        source_pick = one_hot(source_ref[:, at], 0, (fines + 2 * rims, step))
        target_pick = one_hot(target_ref[:, at], 0, (fines, step))
        edge_sum = product(sent_v[...], source_pick) + product(got_v[...], target_pick)
        edge_hidden = gate(edge_sum).astype(bf16)
        edge_v[...] += lax.dot_general(target_pick, edge_hidden, across, preferred_element_type=f32)
        return carry

    lax.fori_loop(0, edges // step, block, 0)
    sums = edge_v[...]
    leading = sums.astype(bf16)
    rest = (sums - leading.astype(f32)).astype(bf16)
    e2 = weight(12)
    aggregate = (product(leading, e2) + product(rest, e2)).astype(bf16)
    hidden = gate(product(lifted, weight(13)) + product(aggregate, weight(14))).astype(bf16)
    fine_out_ref[...] = (lifted.astype(f32) + normed(product(hidden, weight(15)))).astype(bf16)

    @pl.when(tile > 0)
    def _():
        for copy in to_before:
            copy.wait_send()

    @pl.when(tile < tiles - 1)
    def _():
        for copy in to_after:
            copy.wait_send()

    for copy in started:
        copy.wait_send()


def on_device(
    fine_latent,
    mid_latent,
    coarse_latent,
    fine_parent,
    mid_parent,
    halo_rows,
    edge_source,
    edge_target,
    w_child,
    mid_w1,
    mid_w2,
    mid_w3,
    w_coarse,
    coarse_w1,
    coarse_w2,
    coarse_w3,
    w_descend,
    w_fine,
    edge_w_src,
    edge_w_dst,
    edge_w2,
    node_w1,
    node_w2,
    node_w3,
):
    groups, tiles = (lax.axis_size("rhombus"), lax.axis_size("tile"))
    devices = groups * tiles
    fines, features = fine_latent.shape
    mids = mid_latent.shape[0]
    halos = halo_rows.shape[0]
    rims = halos // 2
    coarse_count = coarse_latent.shape[0]
    weights = (
        w_child,
        mid_w1,
        mid_w2,
        mid_w3,
        coarse_w1,
        edge_w_src,
        edge_w_dst,
        w_coarse,
        coarse_w2,
        coarse_w3,
        w_descend,
        w_fine,
        edge_w2,
        node_w1,
        node_w2,
        node_w3,
    )
    ceil = lambda n: -(-n // 128) * 128
    width = ceil(mids)
    coarse_ids = jnp.pad(mid_parent[None, :], ((0, 0), (0, width - mids)))
    pairs = tiles // 2
    level = 2 if pairs == 4 else pairs - 1
    sends = groups + level + (groups - 1) * (level + 1) + groups * level
    sends += 2 * groups if pairs == 4 else 0
    bf16, f32, i32 = (jnp.bfloat16, jnp.float32, jnp.int32)
    vmem = pl.BlockSpec(memory_space=pltpu.VMEM)
    hbm = pl.BlockSpec(memory_space=pl.ANY)
    dma = pltpu.SemaphoreType.DMA
    return pl.pallas_call(
        lambda *refs: sweep_kernel(groups, tiles, *refs),
        out_shape=(
            jax.ShapeDtypeStruct((fines, features), bf16),
            jax.ShapeDtypeStruct((mids, features), bf16),
            jax.ShapeDtypeStruct((coarse_count, features), bf16),
        ),
        in_specs=[vmem] * 7 + [hbm] * (1 + len(weights)),
        out_specs=(vmem, vmem, vmem),
        scratch_shapes=[
            pltpu.VMEM((devices, mids, features), bf16),
            pltpu.VMEM((devices, 1, width), i32),
            pltpu.VMEM((halos, features), bf16),
            pltpu.VMEM((2, 1, rims), i32),
            pltpu.VMEM((fines, features), bf16),
            pltpu.VMEM((len(weights), features, features), bf16),
            pltpu.VMEM((3 * mids, features), f32),
            pltpu.VMEM((2, mids, features), f32),
            pltpu.VMEM((halos, features), bf16),
            pltpu.VMEM((2, 1, rims), i32),
            pltpu.VMEM((coarse_count, features), f32),
            pltpu.VMEM((2, features, features), bf16),
            pltpu.VMEM((coarse_count, features), f32),
            pltpu.VMEM((ceil(coarse_count), features), bf16),
            pltpu.VMEM((ceil(5 * mids), features), bf16),
            pltpu.VMEM((fines + halos, features), bf16),
            pltpu.VMEM((features, fines + halos), bf16),
            pltpu.VMEM((features, fines), bf16),
            pltpu.VMEM((fines, features), f32),
            dma((len(weights) + 1,)),
            dma((6,)),
            dma((6,)),
            dma((2, sends)),
            dma((devices,)),
            dma((devices,)),
        ],
        compiler_params=pltpu.CompilerParams(collective_id=0, has_side_effects=True),
        name="sweep",
    )(
        fine_parent[None, :],
        halo_rows[None, :],
        mid_latent,
        coarse_ids,
        edge_source[None, :],
        edge_target[None, :],
        coarse_latent,
        fine_latent,
        *weights,
    )


def solution(mesh):
    placed = (
        P(("rhombus", "tile"), None),
        P(("rhombus", "tile"), None),
        P(),
        P(("rhombus", "tile")),
        P(("rhombus", "tile")),
        P(("rhombus", "tile")),
        P(("rhombus", "tile")),
        P(("rhombus", "tile")),
        P(),
        P(),
        P(),
        P(),
        P(),
        P(),
        P(),
        P(),
        P(),
        P(),
        P(),
        P(),
        P(),
        P(),
        P(),
        P(),
    )
    return jax.shard_map(
        on_device,
        mesh=mesh,
        in_specs=placed,
        out_specs=(P(("rhombus", "tile"), None), P(("rhombus", "tile"), None), P()),
        check_vma=False,
    )
```
